128 devices in a mesh: tm: 16 (over z, y), mom: 8 (over x, core).
Axes of the slice: x: 4, y: 4, z: 4, core: 2. Of those that a mesh axis runs over, the one named last changes fastest.
Arguments:
- elem_one: bfloat16 [16, 8, 2, 512, 512], P('tm', 'mom'), may hold values from -6 to 6
- elem_two: bfloat16 [16, 8, 2, 512, 512], P('tm', 'mom'), may hold values from -6 to 6
- peramb: bfloat16 [16, 2, 512, 512], P('tm', None, 'mom'), may hold values from -0.1875 to 0.1875
- diagrams: int32 [16, 8, 3, 8], P('tm', 'mom'), may hold values from -2 to 15, as said below
- counts: int32 [16, 8], P('tm', 'mom'), may hold values from 1 to 8, as said below
Outputs:
- correlator: float32 [16, 8, 2, 512, 512], P('tm', 'mom')
The draws below stay inside these ranges and needn't reach their ends.
Inputs may be any that keep to these rules, and one draw needn't show every extreme that they name: `diagrams`: field 0 and field 1 of every slot are timeslices 0 to 15; field 2 is one of -2, -1, 1, 2; slots at or past the count hold such values too. `counts`: some timeslice and momentum has exactly 8 live slots.
All inputs are finite; a program needn't handle non-finite values.
Results may differ from the reference program's by a relative error of at most 0.0075.
Values may be sent and summed in bfloat16 or wider, within the bound.
No kernel may reach another device: no remote copies, remote signals or barrier semaphores. Data moves between devices by JAX's collectives and lax.ppermute only.
A program may use at most 192 MiB of HBM per device.

```python
import math
import jax
import jax.numpy as jnp
from jax import lax

ORDER = 512
DIAG_MAX = 8
N_TM = 16
N_MOM = 8


def draw_diagrams(key, part):
    base_key = jax.random.fold_in(key, 101)
    time_key, owner_key, code_key = jax.random.split(base_key, 3)
    far_time = jax.random.randint(time_key, (N_TM, N_MOM, DIAG_MAX), 0, N_TM, dtype=jnp.int32)
    owner_row = jax.random.randint(owner_key, (N_TM, N_MOM, DIAG_MAX), 0, N_TM, dtype=jnp.int32)
    picked = jax.random.randint(code_key, (N_TM, N_MOM, DIAG_MAX), 0, 4, dtype=jnp.int32)
    weight_code = picked - 2 + (picked >= 2).astype(jnp.int32)
    return jnp.stack([far_time, owner_row, weight_code], axis=2)


def draw_counts(key, part):
    base_key = jax.random.fold_in(key, 202)
    level_key, place_key = jax.random.split(base_key)
    levels = jax.random.randint(level_key, (N_TM * N_MOM,), 0, 4, dtype=jnp.int32)
    flat_counts = jnp.where(levels == 0, DIAG_MAX, 1).astype(jnp.int32)
    chosen = jax.random.randint(place_key, (), 0, N_TM * N_MOM, dtype=jnp.int32)
    flat_counts = jnp.where(jnp.arange(N_TM * N_MOM, dtype=jnp.int32) == chosen, DIAG_MAX, flat_counts)
    return flat_counts.reshape(N_TM, N_MOM)


def shard_levels(own_key, dims, pieces, smallest, largest):
    def one(dim, blocks):
        draws = jax.random.uniform(jax.random.fold_in(jax.random.fold_in(own_key, 6), dim), (blocks,), jnp.float32, smallest / len(pieces), largest / len(pieces))
        return jnp.repeat(jnp.exp(draws), dims[dim] // blocks).reshape((-1,) + (1,) * (len(dims) - dim - 1))

    gain = one(*pieces[0])
    for cut in pieces[1:]:
        gain = gain * one(*cut)
    return gain


def normal_values(key, shape, width, bound, cuts=(), held_as=jnp.bfloat16):
    array = width * jax.random.normal(key, shape, jnp.float32)
    if cuts:
        array = array * shard_levels(key, shape, cuts, -0.22, 0.18)
    return jnp.clip(array, -bound, bound).astype(held_as)


def setup_inputs(seed: int = 0) -> dict:
    arg_keys = jax.random.split(jax.random.key(seed), 6)
    return {
        "elem_one": normal_values(arg_keys[0], (N_TM, N_MOM, 2, ORDER, ORDER), 1.0, 6.0, ((0, 16), (1, 8))),
        "elem_two": normal_values(arg_keys[1], (N_TM, N_MOM, 2, ORDER, ORDER), 1.0, 6.0, ((0, 16), (1, 8))),
        "peramb": normal_values(arg_keys[2], (N_TM, 2, ORDER, ORDER), (2 * ORDER) ** -0.5, 0.1875, ((0, 16), (2, 8))),
        "diagrams": draw_diagrams(jax.random.fold_in(arg_keys[5], 71), 0),
        "counts": draw_counts(jax.random.fold_in(arg_keys[5], 71), 0),
    }


def complex_product(left_node, right_node):
    real_real = jnp.dot(left_node[0], right_node[0], preferred_element_type=jnp.float32)
    imag_imag = jnp.dot(left_node[1], right_node[1], preferred_element_type=jnp.float32)
    real_imag = jnp.dot(left_node[0], right_node[1], preferred_element_type=jnp.float32)
    imag_real = jnp.dot(left_node[1], right_node[0], preferred_element_type=jnp.float32)
    return jnp.stack([real_real - imag_imag, real_imag + imag_real])

def build_nodes(elem_mats, peramb):

    def one_time(inputs):
        elem_time, peramb_time = inputs
        elem_float = elem_time.astype(jnp.float32)
        peramb_float = peramb_time.astype(jnp.float32)
        real_part = jnp.einsum('mij,jk->mik', elem_float[:, 0], peramb_float[0]) - jnp.einsum('mij,jk->mik', elem_float[:, 1], peramb_float[1])
        imag_part = jnp.einsum('mij,jk->mik', elem_float[:, 0], peramb_float[1]) + jnp.einsum('mij,jk->mik', elem_float[:, 1], peramb_float[0])
        return jnp.stack([real_part, imag_part], axis=1).astype(jnp.bfloat16)
    return lax.map(one_time, (elem_mats, peramb))

def reference(elem_one, elem_two, peramb, diagrams, counts):
    nodes_left = build_nodes(elem_one, peramb)
    nodes_right = build_nodes(elem_two, peramb)
    factor = 1.0 / (2.0 * math.sqrt(2.0 * ORDER))

    def per_time(correlator, time_index):
        partial_value = jnp.zeros((N_MOM, N_TM, 2, ORDER, ORDER), jnp.float32)

        def add_slot(flat_index, partial_sum):
            mom_index = flat_index // DIAG_MAX
            slot_index = flat_index % DIAG_MAX
            far_time = diagrams[time_index, mom_index, 0, slot_index]
            owner_row = diagrams[time_index, mom_index, 1, slot_index]
            weight_code = diagrams[time_index, mom_index, 2, slot_index]
            left_node = nodes_left[time_index, mom_index]
            right_node = nodes_right[far_time, mom_index]
            product = lax.cond(slot_index < counts[time_index, mom_index], lambda: complex_product(left_node, right_node) * (weight_code.astype(jnp.float32) * factor), lambda: jnp.zeros((2, ORDER, ORDER), jnp.float32))
            return partial_sum.at[mom_index, owner_row].add(product)
        partial_value = lax.fori_loop(0, N_MOM * DIAG_MAX, add_slot, partial_value)
        rounded = lax.optimization_barrier(partial_value.astype(jnp.bfloat16)).astype(jnp.float32)
        return (correlator + jnp.transpose(rounded, (1, 0, 2, 3, 4)), None)
    start_sum = jnp.zeros((N_TM, N_MOM, 2, ORDER, ORDER), jnp.float32)
    correlator, _ = lax.scan(per_time, start_sum, jnp.arange(N_TM, dtype=jnp.int32))
    return correlator
```

```python
import functools
import math

import jax
import jax.numpy as jnp
from jax import lax
from jax.experimental import pallas as pl
from jax.experimental.pallas import tpu as pltpu
from jax.sharding import PartitionSpec as P


VMEM = pl.BlockSpec(memory_space=pltpu.VMEM)
SMEM = pl.BlockSpec(memory_space=pltpu.SMEM)


def sent_tm(value, dz, dy, side):
    pairs = [
        (z * side + y, (z + dz) % side * side + (y + dy) % side)
        for z in range(side)
        for y in range(side)
    ]
    return lax.ppermute(value, "tm", pairs)


def sent_mom(value, dx, dcore, chips):
    pairs = [
        (2 * x + core, 2 * ((x + dx) % chips) + (core + dcore) % 2)
        for x in range(chips)
        for core in range(2)
    ]
    return lax.ppermute(value, "mom", pairs)


def complex_rows(real_rows, imag_rows, both):
    half = both.shape[1] // 2
    by_real = jnp.dot(real_rows, both, preferred_element_type=jnp.float32)
    by_imag = jnp.dot(imag_rows, both, preferred_element_type=jnp.float32)
    real = by_real[:, :half] - by_imag[:, half:]
    imag = by_real[:, half:] + by_imag[:, :half]
    return real.astype(jnp.bfloat16), imag.astype(jnp.bfloat16)


def right_kernel(place, elem, own, other, *refs, side, chips):
    outs, whole = refs[:side], refs[side]
    y, x, core = place[1], place[2], place[3]
    rows = own.shape[2]
    for d in range(chips):
        chip = lax.rem(x - d + chips, chips)
        for held, c in ((own, core), (other, 1 - core)):
            at = pl.multiple_of((2 * chip + c) * rows, rows)
            whole[:, pl.ds(at, rows), :] = held[d]
    order = elem.shape[1]
    width = order // side
    tall = 128
    for d in range(side):
        at = pl.multiple_of(lax.rem(y + d, side) * width, width)
        both = jnp.concatenate(
            [whole[0, :, pl.ds(at, width)], whole[1, :, pl.ds(at, width)]], axis=1
        )

        def step(n, carry, d=d, both=both):
            part = pl.ds(pl.multiple_of(n * tall, tall), tall)
            real, imag = complex_rows(elem[0, part, :], elem[1, part, :], both)
            outs[d][part, :width] = real
            outs[d][part, width:] = imag
            return carry

        lax.fori_loop(0, order // tall, step, 0)


def left_kernel(place, elem, whole, *outs, side):
    z = place[0]
    order = elem.shape[1]
    height = order // side
    for d in range(side):
        part = pl.ds(pl.multiple_of(lax.rem(z + d, side) * height, height), height)

        def step(n, carry, d=d, part=part):
            columns = pl.ds(pl.multiple_of(n * 128, 128), 128)
            both = jnp.concatenate([whole[0, :, columns], whole[1, :, columns]], axis=1)
            real, imag = complex_rows(elem[0, part, :], elem[1, part, :], both)
            outs[d][:height, columns] = real
            outs[d][height:, columns] = imag
            return carry

        lax.fori_loop(0, order // 128, step, 0)


def slots_kernel(place, lists, *refs, side, slots, factor):
    pieces, (out, left, right, total, table) = refs[:-5], refs[-5:]
    z, y = place[0], place[1]
    l_own, l_down, l_up, l_low, l_high, r_own, r_down, r_up, r_low, r_high = pieces
    half = side // 2

    def kept(dest, source, at, d, group, by_rows):
        a, b = (d, group) if by_rows else (group, d)
        t = lax.rem(z - a + side, side) * side + lax.rem(y - b + side, side)
        dest[t] = source[at]

    for dest, (own, down, up, low, high), by_rows in (
        (left, (l_own, l_down, l_up, l_low, l_high), True),
        (right, (r_own, r_down, r_up, r_low, r_high), False),
    ):
        for d in range(side):
            kept(dest, own, d, d, 0, by_rows)
            kept(dest, down, d, d, 1, by_rows)
            kept(dest, up, d, d, side - 1, by_rows)
        for d in range(half):
            kept(dest, low, d, d, 2, by_rows)
            kept(dest, high, d, d + half, 2, by_rows)

    devices = side * side

    def clear(o, carry):
        total[o] = jnp.zeros(total.shape[1:], jnp.float32)
        return carry

    lax.fori_loop(0, devices, clear, 0)

    def list_time(t, at):
        def list_slot(s, where):
            table[0, where] = t
            table[1, where] = lists[t, s]
            table[2, where] = lists[t, slots + s]
            table[3, where] = lists[t, 2 * slots + s]
            return where + 1

        return lax.fori_loop(0, lists[t, 3 * slots], list_slot, at)

    live = lax.fori_loop(0, devices, list_time, 0)
    height, width = total.shape[2], total.shape[3]

    def add_slot(n, carry):
        t, b, o = table[0, n], table[1, n], table[2, n]
        code = table[3, n].astype(jnp.float32)
        product = jnp.dot(left[t], right[b], preferred_element_type=jnp.float32)
        real = product[:height, :width] - product[height:, width:]
        imag = product[:height, width:] + product[height:, :width]
        total[o, 0] += code * real
        total[o, 1] += code * imag
        return carry

    lax.fori_loop(0, live, add_slot, 0)

    def finish(o, carry):
        out[o] = (total[o] * factor).astype(jnp.bfloat16)
        return carry

    lax.fori_loop(0, devices, finish, 0)


def place_kernel(blocks, out):
    width = blocks.shape[-1]
    for j in range(blocks.shape[0]):
        out[:, :, j * width : (j + 1) * width] = blocks[j].astype(jnp.float32)


def local(side, chips, elem_one, elem_two, peramb, diagrams, counts):
    order = elem_one.shape[-1]
    slots = diagrams.shape[-1]
    devices = side * side
    block = order // side
    factor = 1.0 / (2.0 * math.sqrt(2.0 * order))
    tm, mom = lax.axis_index("tm"), lax.axis_index("mom")
    place = jnp.stack([tm // side, tm % side, mom // 2, mom % 2]).astype(jnp.int32)

    own = peramb[0]
    down = sent_mom(own, 1, 0, chips)
    up = sent_mom(own, -1, 0, chips)
    across = sent_mom(own, 2, 0, chips)
    mine = jnp.stack([own, down, across, up])
    theirs = sent_mom(mine, 0, 1, chips)

    listed = jnp.concatenate([diagrams.reshape(1, -1), counts.reshape(1, 1)], axis=1)
    listed = jnp.pad(listed, ((0, 0), (0, 128 - listed.shape[1])))
    for dz, dy in ((1, 0), (0, 1)):
        listed = jnp.stack(
            [listed] + [sent_tm(listed, d * dz, d * dy, side) for d in range(1, side)]
        )
    back_z = (place[0] - jnp.arange(side)) % side
    back_y = (place[1] - jnp.arange(side)) % side
    listed = listed.reshape(side, side, 128)[back_y][:, back_z]
    listed = jnp.swapaxes(listed, 0, 1).reshape(devices, 128)

    bf16 = lambda *shape: jax.ShapeDtypeStruct(shape, jnp.bfloat16)
    limit = pltpu.CompilerParams(vmem_limit_bytes=24 << 20)
    *rights, whole = pl.pallas_call(
        functools.partial(right_kernel, side=side, chips=chips),
        out_shape=[bf16(order, 2 * block)] * side + [bf16(2, order, order)],
        in_specs=[SMEM] + [VMEM] * 3,
        out_specs=[VMEM] * (side + 1),
        compiler_params=limit,
        name="right_nodes",
    )(place, elem_two[0, 0], mine, theirs)
    lefts = pl.pallas_call(
        functools.partial(left_kernel, side=side),
        out_shape=[bf16(2 * block, order)] * side,
        in_specs=[SMEM] + [VMEM] * 2,
        out_specs=[VMEM] * side,
        compiler_params=limit,
        name="left_nodes",
    )(place, elem_one[0, 0], whole)

    def spread(blocks, first, second):
        came = [blocks[0]]
        came += [sent_tm(blocks[d], *(d * a for a in first), side) for d in range(1, side)]
        held = jnp.stack(came)
        below = sent_tm(held, *second, side)
        above = sent_tm(held, *(-a for a in second), side)
        low = sent_tm(below[: side // 2], *second, side)
        high = sent_tm(above[side // 2 :], *(-a for a in second), side)
        return [held, below, above, low, high]

    right_pieces = spread(rights, (0, 1), (1, 0))
    left_pieces = spread(lefts, (1, 0), (0, 1))

    blocks = pl.pallas_call(
        functools.partial(slots_kernel, side=side, slots=slots, factor=factor),
        out_shape=bf16(devices, 2, block, block),
        in_specs=[SMEM] * 2 + [VMEM] * 10,
        out_specs=VMEM,
        scratch_shapes=[
            pltpu.VMEM((devices, 2 * block, order), jnp.bfloat16),
            pltpu.VMEM((devices, order, 2 * block), jnp.bfloat16),
            pltpu.VMEM((devices, 2, block, block), jnp.float32),
            pltpu.SMEM((4, devices * slots), jnp.int32),
        ],
        compiler_params=pltpu.CompilerParams(vmem_limit_bytes=32 << 20),
        name="slots",
    )(place, listed, *left_pieces, *right_pieces)
    arrived = lax.all_to_all(blocks, "tm", 0, 0, tiled=True)
    correlator = pl.pallas_call(
        place_kernel,
        out_shape=jax.ShapeDtypeStruct((2, order, order), jnp.float32),
        grid=(side,),
        in_specs=[pl.BlockSpec((side, 2, block, block), lambda i: (i, 0, 0, 0))],
        out_specs=pl.BlockSpec((2, block, order), lambda i: (0, i, 0)),
        name="placed",
    )(arrived)
    return correlator[None, None]


def solution(mesh):
    side = math.isqrt(mesh.shape["tm"])
    return jax.shard_map(
        functools.partial(local, side, mesh.shape["mom"] // 2),
        mesh=mesh,
        in_specs=(
            P("tm", "mom", None, None, None),
            P("tm", "mom", None, None, None),
            P("tm", None, "mom", None),
            P("tm", "mom", None, None),
            P("tm", "mom"),
        ),
        out_specs=P("tm", "mom", None, None, None),
        check_vma=False,
    )
```
